32 devices in a mesh: dp: 8 (over z, y), tp: 4 (over x, core).
Axes of the slice: x: 2, y: 2, z: 4, core: 2. Of those that a mesh axis runs over, the one named last changes fastest.
Arguments:
- hidden: bfloat16 [16, 4096], P('dp'), may hold values from -6 to 6
- attention_norm_gain: bfloat16 [4096], replicated, may hold values from 0.5 to 1.5
- query_key_value_weight: bfloat16 [4096, 4, 1280], P('dp', 'tp'), may hold values from -0.09375 to 0.09375
- key_value_cache: bfloat16 [16, 2048, 4, 256], P('dp', None, 'tp'), may hold values from -6 to 6
- cache_fill_lengths: int32 [16], P('dp'), may hold values from 2 to 2048
- output_weight_frozen: bfloat16 [4, 1024, 4096], P('tp', None, 'dp'), may hold values from -0.09375 to 0.09375
- adapter_down_transposed: bfloat16 [64, 4, 1024], P(None, 'tp', 'dp'), may hold values from -0.09375 to 0.09375
- adapter_up_matrix: bfloat16 [64, 4, 1024], P(None, 'tp', 'dp'), may hold values from -0.75 to 0.75
- attention_rows: bfloat16 [4096, 4096], P('dp', 'tp'), may hold values from -6 to 6
- upstream: bfloat16 [4096, 4096], P('dp', 'tp'), may hold values from -6 to 6
- rewards: float32 [16], P('dp'), may hold values from 0 to 2
- prompt_group_index: int32 [16], P('dp'), may hold values from 0 to 3, as said below
- completion_live_lengths: int32 [16], P('dp'), may hold values from 1 to 256
Outputs:
- decoded: float32 [16, 4096], P('dp')
- adapted_output_rows: float32 [4096, 4096], P('dp', 'tp')
- grad_lora_a_t: float32 [64, 4, 1024], P(None, 'tp', 'dp')
- grad_lora_b: float32 [64, 4, 1024], P(None, 'tp', 'dp')
The draws below stay inside these ranges and needn't reach their ends.
Inputs may be any that keep to these rules, and one draw needn't show every extreme that they name: `prompt_group_index`: each prompt holds exactly 4 rollouts.
All inputs are finite; a program needn't handle non-finite values.
Results may differ from the reference program's by a relative error of at most 0.0041.
Values may be sent and summed in bfloat16 or wider, within the bound.
A program may use at most 128 MiB of HBM per device.

```python
import math
import jax
import jax.numpy as jnp
from jax import lax

MODEL_WIDTH = 4096
HD = 128
HEADS_TP = 8
ADAPTER_RANK = 64
CTX = 2048
GROUP = 4
COMP = 256
ROLLOUTS = 16
GROUP_QUERY_DIMS = 1024
QKV_TP = 1280
SHARD_WIDTH = 1024
ROWS = 4096
N_TP = 4


def draw_prompt_group_index(key, part):
    order = jax.random.permutation(key, ROLLOUTS)
    return (order // GROUP).astype(jnp.int32)


def draw_query_key_value_weight(key, part):
    noise_key = jax.random.fold_in(key, 101)
    weight = jax.random.truncated_normal(noise_key, -6.0, 6.0, (MODEL_WIDTH, N_TP, QKV_TP), jnp.float32) / math.sqrt(MODEL_WIDTH)
    return weight.astype(jnp.bfloat16)


def draw_key_value_cache(key, part):
    cache = jax.random.truncated_normal(jax.random.fold_in(key, 202), -6.0, 6.0, (ROLLOUTS, CTX, N_TP, 2 * HD), jnp.float32)
    return cache.astype(jnp.bfloat16)


def set_ends(entries, rng, low, high):
    place = [jax.random.randint(jax.random.fold_in(rng, axis), (), 0, length) for axis, length in enumerate(entries.shape)]
    main_axis = entries.shape.index(max(entries.shape))
    neighbour = place[:main_axis] + [(place[main_axis] + 1) % entries.shape[main_axis]] + place[main_axis + 1:]
    return entries.at[tuple(place)].set(low).at[tuple(neighbour)].set(high)


def shard_levels(key, extent, cuts, least, high):
    def one(dim, shards_of):
        steps = jax.random.uniform(jax.random.fold_in(jax.random.fold_in(key, 6), dim), (shards_of,), jnp.float32, least / len(cuts), high / len(cuts))
        return jnp.repeat(jnp.exp(steps), extent[dim] // shards_of).reshape((-1,) + (1,) * (len(extent) - dim - 1))

    level = one(*cuts[0])
    for cut in cuts[1:]:
        level = level * one(*cut)
    return level


def gaussian(stream_key, shape, spread, bound, cuts=(), held_as=jnp.bfloat16):
    level = shard_levels(stream_key, shape, cuts, -0.22, 0.18) if cuts else 1.0
    array = jax.random.normal(stream_key, shape, jnp.float32) * spread * level
    return jnp.minimum(jnp.maximum(array, -bound), bound).astype(held_as)


def setup_inputs(seed: int = 0) -> dict:
    seeds = jax.random.split(jax.random.key(seed), 14)
    hidden = gaussian(seeds[0], (ROLLOUTS, MODEL_WIDTH), 1.0, 6.0, ((0, 8),))
    attention_norm_gain = jnp.clip(1.0 + 0.1 * jax.random.normal(seeds[1], (MODEL_WIDTH,), jnp.float32), 0.5, 1.5).astype(jnp.bfloat16)
    query_key_value_weight = draw_query_key_value_weight(jax.random.fold_in(seeds[13], 71), 0)
    key_value_cache = draw_key_value_cache(jax.random.fold_in(seeds[13], 71), 0)
    cache_fill_lengths = set_ends(jax.random.randint(seeds[4], (ROLLOUTS,), 2, CTX + 1), jax.random.fold_in(seeds[4], 1), 2, CTX).astype(jnp.int32)
    output_weight_frozen = gaussian(seeds[5], (N_TP, GROUP_QUERY_DIMS, MODEL_WIDTH), (GROUP_QUERY_DIMS * N_TP) ** -0.5, 0.09375, ((0, 4), (2, 8)))
    adapter_down_transposed = gaussian(seeds[6], (ADAPTER_RANK, N_TP, GROUP_QUERY_DIMS), (GROUP_QUERY_DIMS * N_TP) ** -0.5, 0.09375, ((1, 4), (2, 8)))
    adapter_up_matrix = gaussian(seeds[7], (ADAPTER_RANK, N_TP, SHARD_WIDTH), ADAPTER_RANK ** -0.5, 0.75, ((1, 4), (2, 8)))
    attention_rows = gaussian(seeds[8], (ROWS, GROUP_QUERY_DIMS * N_TP), 1.0, 6.0, ((0, 8), (1, 4)))
    upstream = gaussian(seeds[9], (ROWS, MODEL_WIDTH), 1.0, 6.0, ((0, 8), (1, 4)))
    rewards = jnp.clip(2.0 * jax.random.uniform(seeds[10], (ROLLOUTS,), jnp.float32) ** shard_levels(seeds[10], (ROLLOUTS,), ((0, 8),), -0.2, 0.2), 0.0, 2.0)
    prompt_group_index = draw_prompt_group_index(jax.random.fold_in(seeds[13], 71), 0)
    completion_live_lengths = set_ends(jax.random.randint(seeds[12], (ROLLOUTS,), 1, COMP + 1), jax.random.fold_in(seeds[12], 1), 1, COMP).astype(jnp.int32)
    return {"hidden": hidden, "attention_norm_gain": attention_norm_gain, "query_key_value_weight": query_key_value_weight, "key_value_cache": key_value_cache, "cache_fill_lengths": cache_fill_lengths, "output_weight_frozen": output_weight_frozen, "adapter_down_transposed": adapter_down_transposed, "adapter_up_matrix": adapter_up_matrix, "attention_rows": attention_rows, "upstream": upstream, "rewards": rewards, "prompt_group_index": prompt_group_index, "completion_live_lengths": completion_live_lengths}


adapter_scale = 2.0

def rms_norm(decode_state, gain):
    scale = lax.rsqrt(lax.optimization_barrier(jnp.mean(decode_state * decode_state, axis=-1, keepdims=True)) + 1e-05)
    return decode_state * scale * gain.astype(jnp.float32)

def one_rollout(packed):
    query, cache, length, new_keys, new_values = packed
    head = query.shape[-1]
    slots = cache.shape[0]
    factor = 1.0 / math.sqrt(head)
    q32 = query.astype(jnp.float32)
    keys = cache[:, :, :head].astype(jnp.float32)
    values = cache[:, :, head:].astype(jnp.float32)
    scores = jnp.einsum('thd,ctd->thc', q32, keys, precision=lax.Precision.HIGHEST) * factor
    valid = jnp.arange(slots) < length
    scores = jnp.where(valid[None, None, :], scores, -1e+30)
    extra = jnp.einsum('thd,etd->the', q32, new_keys.astype(jnp.float32), precision=lax.Precision.HIGHEST) * factor
    joined = jnp.concatenate([scores, extra], axis=-1)
    top = lax.optimization_barrier(jnp.max(joined, axis=-1, keepdims=True))
    expo = jnp.exp(joined - top)
    probs = (expo / lax.optimization_barrier(jnp.sum(expo, axis=-1, keepdims=True))).astype(jnp.bfloat16).astype(jnp.float32)
    out = jnp.einsum('thc,ctd->thd', probs[..., :slots], values, precision=lax.Precision.HIGHEST)
    out = out + jnp.einsum('the,etd->thd', probs[..., slots:], new_values.astype(jnp.float32), precision=lax.Precision.HIGHEST)
    return out.astype(jnp.bfloat16)

def reference(hidden, attention_norm_gain, query_key_value_weight, key_value_cache, cache_fill_lengths, output_weight_frozen, adapter_down_transposed, adapter_up_matrix, attention_rows, upstream, rewards, prompt_group_index, completion_live_lengths):
    rollouts = hidden.shape[0]
    w_qkv = query_key_value_weight.reshape(MODEL_WIDTH, N_TP * QKV_TP).astype(jnp.float32)
    w_out = output_weight_frozen.reshape(N_TP * GROUP_QUERY_DIMS, MODEL_WIDTH)
    down_matrix_full = adapter_down_transposed.reshape(ADAPTER_RANK, N_TP * GROUP_QUERY_DIMS)
    up_matrix_full = adapter_up_matrix.reshape(ADAPTER_RANK, MODEL_WIDTH)
    decode_state = hidden.astype(jnp.float32)
    keys_new = []
    values_new = []
    for step in range(2):
        normed = rms_norm(decode_state, attention_norm_gain)
        qkv = jnp.dot(normed, w_qkv, precision=lax.Precision.HIGHEST)
        qkv = qkv.reshape(rollouts, N_TP, QKV_TP)
        query = qkv[:, :, :GROUP_QUERY_DIMS].reshape(rollouts, N_TP, HEADS_TP, HD)
        keys_new.append(qkv[:, :, GROUP_QUERY_DIMS:GROUP_QUERY_DIMS + HD])
        values_new.append(qkv[:, :, GROUP_QUERY_DIMS + HD:])
        stacked_k = jnp.stack(keys_new, axis=1)
        stacked_v = jnp.stack(values_new, axis=1)
        attended = lax.map(one_rollout, (query, key_value_cache, cache_fill_lengths, stacked_k, stacked_v))
        attended = attended.reshape(rollouts, N_TP * GROUP_QUERY_DIMS)
        frozen_output = jnp.dot(attended, w_out, preferred_element_type=jnp.float32)
        low_rank_decode = jnp.dot(attended, down_matrix_full.T, preferred_element_type=jnp.float32)
        decode_state = decode_state + frozen_output + adapter_scale * jnp.dot(low_rank_decode, up_matrix_full.astype(jnp.float32), precision=lax.Precision.HIGHEST)
    decoded = decode_state
    groups = rollouts // GROUP
    onehot = (prompt_group_index[:, None] == jnp.arange(groups, dtype=jnp.int32)[None, :]).astype(jnp.float32)
    totals = lax.optimization_barrier(jnp.sum(onehot * rewards[:, None], axis=0))
    squares = lax.optimization_barrier(jnp.sum(onehot * (rewards * rewards)[:, None], axis=0))
    mean = totals / GROUP
    std = jnp.sqrt(jnp.maximum(squares / GROUP - mean * mean, 0.09))
    advantage = (rewards - lax.optimization_barrier(jnp.sum(onehot * mean[None, :], axis=1))) / lax.optimization_barrier(jnp.sum(onehot * std[None, :], axis=1))
    per_roll = advantage / completion_live_lengths.astype(jnp.float32)
    rows = attention_rows.shape[0]
    slot = jnp.arange(rows, dtype=jnp.int32) % COMP
    limit = jnp.repeat(completion_live_lengths, COMP)
    row_w = jnp.where(slot < limit, jnp.repeat(per_roll, COMP), 0.0)
    low_rank_rows = jnp.dot(attention_rows, down_matrix_full.T, preferred_element_type=jnp.float32).astype(jnp.bfloat16)
    frozen_output_rows = jnp.dot(attention_rows, w_out, preferred_element_type=jnp.float32)
    adapted_output_rows = frozen_output_rows + adapter_scale * jnp.dot(low_rank_rows, up_matrix_full, preferred_element_type=jnp.float32)
    advantage_weighted = (row_w[:, None] * upstream.astype(jnp.float32)).astype(jnp.bfloat16)
    backward_result = jnp.dot(advantage_weighted, up_matrix_full.T, preferred_element_type=jnp.float32).astype(jnp.bfloat16)
    down_gradient = adapter_scale * lax.dot_general(backward_result, attention_rows, (((0,), (0,)), ((), ())), preferred_element_type=jnp.float32)
    up_gradient = adapter_scale * lax.dot_general(low_rank_rows, advantage_weighted, (((0,), (0,)), ((), ())), preferred_element_type=jnp.float32)
    return (decoded, adapted_output_rows, down_gradient.reshape(ADAPTER_RANK, N_TP, GROUP_QUERY_DIMS), up_gradient.reshape(ADAPTER_RANK, N_TP, MODEL_WIDTH // N_TP))
```

```python
import math

import jax
import jax.numpy as jnp
from jax import lax
from jax.experimental import pallas as pl
from jax.experimental.pallas import tpu as pltpu
from jax.sharding import PartitionSpec as P

HD = 128
HEADS_TP = 8
GROUP = 4
COMP = 256


adapter_scale = 2.0


def rms_norm(decode_state, gain):
    scale = lax.rsqrt(jnp.mean(decode_state * decode_state, axis=-1, keepdims=True) + 1e-05)
    return decode_state * scale * gain.astype(jnp.float32)


def attend(query, cache, lengths, new_keys, new_values):
    head = query.shape[-1]
    slots = cache.shape[1]
    factor = 1.0 / math.sqrt(head)
    keys = cache[:, :, :head].astype(jnp.float32)
    values = cache[:, :, head:]
    scores = jnp.einsum("bhd,bcd->bhc", query, keys, precision=lax.Precision.HIGHEST) * factor
    valid = jnp.arange(slots, dtype=jnp.int32)[None, None, :] < lengths[:, None, None]
    scores = jnp.where(valid, scores, -1e30)
    extra = jnp.einsum("bhd,bed->bhe", query, new_keys, precision=lax.Precision.HIGHEST) * factor
    joined = jnp.concatenate([scores, extra], axis=-1)
    top = jnp.max(joined, axis=-1, keepdims=True)
    expo = jnp.exp(joined - top)
    probs = (expo / jnp.sum(expo, axis=-1, keepdims=True)).astype(jnp.bfloat16)
    out = jnp.einsum("bhc,bcd->bhd", probs[..., :slots], values, preferred_element_type=jnp.float32)
    out = out + jnp.einsum(
        "bhe,bed->bhd",
        probs[..., slots:].astype(jnp.float32),
        new_values,
        precision=lax.Precision.HIGHEST,
    )
    return out.astype(jnp.bfloat16).reshape(query.shape[0], -1)


MESH = pl.DeviceIdType.MESH
F32 = jnp.float32
BF16 = jnp.bfloat16
NT = (((1,), (1,)), ((), ()))
TN = (((0,), (0,)), ((), ()))
CHUNK = 256


def split3(v):
    hi = v.astype(BF16)
    rest = v - hi.astype(F32)
    mid = rest.astype(BF16)
    lo = (rest - mid.astype(F32)).astype(BF16)
    return jnp.concatenate([hi, mid, lo], axis=0)


def exact_dot(v, w, dims=(((1,), (0,)), ((), ()))):
    n = v.shape[0]
    r = lax.dot_general(split3(v), w, dims, preferred_element_type=F32)
    return r[:n] + r[n : 2 * n] + r[2 * n :]


def rows_of(ref, n):
    return jnp.concatenate([ref[i] for i in range(n)], axis=0)


def lanes_of(ref, n):
    return jnp.concatenate([ref[i] for i in range(n)], axis=1)


def fused_kernel(
    ndp,
    ntp,
    h_ref,
    gain_ref,
    wqkv_ref,
    cache_ref,
    lens_ref,
    wo_ref,
    a_ref,
    b_ref,
    x_ref,
    up_ref,
    stats_ref,
    dec_ref,
    out_ref,
    ga_ref,
    gb_ref,
    hbuf,
    abuf,
    bbuf,
    bdbuf,
    statbuf,
    qsend,
    qrecv,
    asend,
    arecv,
    usend,
    urecv,
    fsend,
    frecv,
    lbsend,
    lbrecv,
    gsend,
    grecv,
    wt_ref,
    xbuf,
    wbuf,
    pbuf,
    prcv,
    ds_s,
    ds_r,
    ts_s,
    ts_r,
    bd_s,
    bd_r,
    xs_s,
    xs_r,
    wl_s,
    wl_r,
    wf_s,
    wf_r,
    ps_s,
    ps_r,
    loc,
):
    d = lax.axis_index("dp")
    t = lax.axis_index("tp")
    z, y = d // 2, d % 2
    x, c = t // 2, t % 2
    nz = ndp // 2
    rolls = h_ref.shape[1]
    width = h_ref.shape[2]
    model = ndp * width
    rank = a_ref.shape[0]
    piece = a_ref.shape[1]
    chunks = wo_ref.shape[1] // CHUNK
    qkvw = wqkv_ref.shape[1]
    rows = x_ref.shape[0]

    barrier = pltpu.get_barrier_semaphore()
    for i in range(ndp):
        for j in range(ntp):
            if i or j:
                pl.semaphore_signal(
                    barrier,
                    inc=1,
                    device_id=((d + i) % ndp, (t + j) % ntp),
                    device_id_type=MESH,
                )
    pl.semaphore_wait(barrier, ndp * ntp - 1)

    sent = []

    def send(src, dst, s, r, dev):
        cp = pltpu.make_async_remote_copy(
            src_ref=src, dst_ref=dst, send_sem=s, recv_sem=r, device_id=dev, device_id_type=MESH
        )
        return cp

    def dp_start(e, src, dst):
        for off in range(1, ndp):
            peer = (d + off) % ndp
            cp = send(src(peer), dst.at[d], ds_s.at[e, off], ds_r.at[e, off], (peer, t))
            cp.start()
            sent.append(cp)

    def dp_wait(e, src, dst):
        for off in range(1, ndp):
            frm = (d + ndp - off) % ndp
            send(src(d), dst.at[frm], ds_s.at[e, off], ds_r.at[e, off], (frm, t)).wait_recv()

    def tp_start(e, src, dst):
        for off in range(1, ntp):
            peer = (t + off) % ntp
            cp = send(src, dst.at[t], ts_s.at[e, off], ts_r.at[e, off], (d, peer))
            cp.start()
            sent.append(cp)

    def tp_wait(e, src, dst):
        for off in range(1, ntp):
            frm = (t + ntp - off) % ntp
            send(src, dst.at[frm], ts_s.at[e, off], ts_r.at[e, off], (d, frm)).wait_recv()

    dp_start(0, lambda p: h_ref.at[p], hbuf)
    hbuf[d] = h_ref[d]
    dp_start(1, lambda p: a_ref, abuf)
    abuf[d] = a_ref[...]
    dp_start(2, lambda p: b_ref, bbuf)
    bbuf[d] = b_ref[...]
    dp_start(3, lambda p: stats_ref, statbuf)
    statbuf[d] = stats_ref[...]
    per = width // piece
    half = ndp // per
    bdst = t * half + d // per
    bslot = d % per
    for j in range(ntp):
        tj = (t + j) % ntp
        if j == 0:
            here = bdst == d

            @pl.when(here)
            def _():
                bdbuf[bslot] = b_ref[...]

            @pl.when(jnp.logical_not(here))
            def _():
                send(b_ref, bdbuf.at[bslot], bd_s.at[0], bd_r.at[bslot], (bdst, tj)).start()

        else:
            cp = send(b_ref, bdbuf.at[bslot], bd_s.at[j], bd_r.at[bslot], (bdst, tj))
            cp.start()
            sent.append(cp)
    mate = 2 * x + (1 - c)
    xcp = send(x_ref, xbuf.at[c], xs_s.at[0], xs_r.at[0], (d, mate))
    xcp.start()
    sent.append(xcp)
    xbuf[c] = x_ref[...]

    dp_wait(0, lambda p: h_ref.at[p], hbuf)
    state = rows_of(hbuf, ndp)
    gain = gain_ref[d]
    new_k, new_v = [], []
    factor = 1.0 / math.sqrt(HD)

    def line_sends(go):
        for ch in range(chunks):
            for off in range(nz):
                zt = (z + off) % nz
                cp = send(
                    wo_ref.at[:, pl.ds(ch * CHUNK, CHUNK)],
                    wbuf.at[z // 2, y, c, ch],
                    wl_s.at[ch, off],
                    wl_r.at[z // 2, c, ch],
                    (2 * zt + y, 2 * x + z % 2),
                )
                if off == 0:

                    @pl.when(z % 2 != c)
                    def _():
                        if go:
                            cp.start()
                        else:
                            cp.wait_send()

                    if go:

                        @pl.when(z % 2 == c)
                        def _():
                            lc = pltpu.make_async_copy(
                                wo_ref.at[:, pl.ds(ch * CHUNK, CHUNK)],
                                wbuf.at[z // 2, y, c, ch],
                                loc.at[ch],
                            )
                            lc.start()
                            lc.wait()

                elif go:
                    cp.start()
                else:
                    cp.wait_send()

    for step in range(2):
        squares = jnp.sum(state * state, axis=-1, keepdims=True)
        part = exact_dot(state * gain, wqkv_ref[...])
        both = jnp.concatenate([part, jnp.broadcast_to(squares, (ndp * rolls, 128))], axis=1)
        for i in range(ndp):
            qsend[step, i] = both[i * rolls : (i + 1) * rolls]
        dp_start(4 + 2 * step, lambda p: qsend.at[step, p], qrecv.at[step])
        qrecv[step, d] = qsend[step, d]
        if step == 0:
            dp_wait(1, lambda p: a_ref, abuf)
            at = lanes_of(abuf, ndp)
            dp_wait(2, lambda p: b_ref, bbuf)
            bt = lanes_of(bbuf, ndp)
            dp_wait(3, lambda p: stats_ref, statbuf)
            tot = statbuf[0]
            for i in range(1, ndp):
                tot = tot + statbuf[i]
            mean = tot[0:1] / GROUP
            std = jnp.sqrt(jnp.maximum(tot[1:2] / GROUP - mean * mean, 0.09))
            for r in range(rolls):
                one = stats_ref[2 + r : 3 + r]
                rew = stats_ref[2 + rolls + r : 3 + rolls + r, 0:1]
                live = stats_ref[2 + 2 * rolls + r : 3 + 2 * rolls + r, 0:1]
                adv = (rew - jnp.sum(one * mean, axis=1, keepdims=True)) / jnp.sum(
                    one * std, axis=1, keepdims=True
                )
                slot = lax.broadcasted_iota(jnp.int32, (COMP, 1), 0).astype(F32)
                row_w = jnp.where(slot < live, adv / live, 0.0)
                seg = pl.ds(r * COMP, COMP)
                wt_ref[seg, :] = (row_w * up_ref[seg, :].astype(F32)).astype(BF16)
            lbsend[0] = lax.dot_general(at, x_ref[...], NT, preferred_element_type=F32)
            lbsend[1] = lax.dot_general(bt, wt_ref[...], NT, preferred_element_type=F32)
        dp_wait(4 + 2 * step, lambda p: qsend.at[step, p], qrecv.at[step])
        total = qrecv[step, 0]
        for i in range(1, ndp):
            total = total + qrecv[step, i]
        qkv = total[:, :qkvw] * lax.rsqrt(total[:, qkvw : qkvw + 1] / model + 1e-05)
        new_k.append(qkv[:, HEADS_TP * HD : HEADS_TP * HD + HD])
        new_v.append(qkv[:, HEADS_TP * HD + HD :])
        for b in range(rolls):
            q = jnp.concatenate(
                [qkv[b : b + 1, h * HD : (h + 1) * HD] for h in range(HEADS_TP)], axis=0
            )
            scores = exact_dot(q, cache_ref[b, :, :HD], NT) * factor
            pos = lax.broadcasted_iota(jnp.int32, scores.shape, 1)
            scores = jnp.where(pos < lens_ref[b], scores, -1e30)
            extra = [
                jnp.sum(q * k[b : b + 1], axis=-1, keepdims=True) * factor for k in new_k
            ]
            top = jnp.max(scores, axis=-1, keepdims=True)
            for e in extra:
                top = jnp.maximum(top, e)
            expo = jnp.exp(scores - top)
            ee = [jnp.exp(e - top) for e in extra]
            den = jnp.sum(expo, axis=-1, keepdims=True)
            for e in ee:
                den = den + e
            att = jnp.dot(
                (expo / den).astype(BF16), cache_ref[b, :, HD:], preferred_element_type=F32
            )
            for e, v in zip(ee, new_v):
                att = att + (e / den).astype(BF16).astype(F32) * v[b : b + 1]
            att = att.astype(BF16).astype(F32)
            asend[step, b : b + 1, :] = jnp.concatenate(
                [att[h : h + 1] for h in range(HEADS_TP)], axis=1
            )
        dp_start(5 + 2 * step, lambda p: asend.at[step], arecv.at[step])
        arecv[step, d] = asend[step]
        if step == 0:
            tp_start(2, lbsend, lbrecv)
            lbrecv[t] = lbsend[...]
        else:
            tp_wait(2, lbsend, lbrecv)
            lb = lbrecv[0]
            for i in range(1, ntp):
                lb = lb + lbrecv[i]
            lb = lb.astype(BF16)
            low_t, back_t = lb[0], lb[1]
            ga = adapter_scale * jnp.dot(back_t, x_ref[...], preferred_element_type=F32)
            gb = adapter_scale * jnp.dot(low_t, wt_ref[...], preferred_element_type=F32)
            for i in range(ndp):
                gsend[i, 0] = ga[:, i * piece : (i + 1) * piece]
                gsend[i, 1] = gb[:, i * piece : (i + 1) * piece]
        dp_wait(5 + 2 * step, lambda p: asend.at[step], arecv.at[step])
        attended = rows_of(arecv.at[step], ndp).astype(BF16)
        usend[step, :, :width] = jnp.dot(attended, wo_ref[...], preferred_element_type=F32)
        usend[step, :, width:] = jnp.concatenate(
            [
                lax.dot_general(attended, at, NT, preferred_element_type=F32),
                jnp.zeros((ndp * rolls, 128 - rank), F32),
            ],
            axis=1,
        )
        tp_start(step, usend.at[step], urecv.at[step])
        urecv[step, t] = usend[step]
        if step == 0:
            src_t = d // half
            for j in range(per):
                frm = (d % half) * per + j
                same = jnp.logical_and(src_t == t, frm == d)

                @pl.when(jnp.logical_not(same))
                def _():
                    send(b_ref, bdbuf.at[j], bd_s.at[0], bd_r.at[j], (frm, src_t)).wait_recv()

            bd = lanes_of(bdbuf, per)
        tp_wait(step, usend.at[step], urecv.at[step])
        upd = urecv[step, 0]
        for i in range(1, ntp):
            upd = upd + urecv[step, i]
        state = state + (
            upd[:, :width] + adapter_scale * exact_dot(upd[:, width : width + rank], bd)
        )

    for i in range(ndp):
        fsend[i] = state[i * rolls : (i + 1) * rolls]
    dp_start(8, lambda p: fsend.at[p], frecv)
    frecv[d] = fsend[d]
    dp_start(9, lambda p: gsend.at[p], grecv)
    grecv[d] = gsend[d]
    line_sends(True)
    out_ref[...] = adapter_scale * lax.dot_general(low_t, bt, TN, preferred_element_type=F32)
    xcp.wait_recv()
    dp_wait(8, lambda p: fsend.at[p], frecv)
    for i in range(ndp):
        dec_ref[:, i * width : (i + 1) * width] = frecv[i]

    other_y = 2 * z + (1 - y)
    other_x = 2 * (1 - x) + c

    def forward(zz, cc, ch):
        return send(
            wbuf.at[zz, y, cc, ch],
            wbuf.at[zz, y, cc, ch],
            wf_s.at[zz, cc, ch],
            wf_r.at[zz, cc, ch],
            (other_y, t),
        )

    def forwarded(zz, cc, ch):
        return send(
            wbuf.at[zz, y, cc, ch],
            wbuf.at[zz, 1 - y, cc, ch],
            wf_s.at[zz, cc, ch],
            wf_r.at[zz, cc, ch],
            (other_y, t),
        )

    def share(yy, ch):
        return send(
            pbuf.at[yy, ch], prcv.at[yy, ch], ps_s.at[yy, ch], ps_r.at[yy, ch], (d, other_x)
        )

    def block(zi, zz, yy, ch):
        p = jnp.dot(xbuf[0], wbuf[zz, yy, 0, ch], preferred_element_type=F32)
        p = p + jnp.dot(xbuf[1], wbuf[zz, yy, 1, ch], preferred_element_type=F32)

        @pl.when(zi == 0)
        def _():
            pbuf[yy, ch] = p
            share(yy, ch).start()

        @pl.when(zi == 1)
        def _():
            cols = pl.ds(pl.multiple_of(yy * chunks * CHUNK + ch * CHUNK, CHUNK), CHUNK)
            out_ref[:, cols] += p

    def turn(q):
        zi = q % 2
        return zi, jnp.where(zi == 0, 1 - x, x), q // 2

    def stage(q, _):
        @pl.when(q < 2 * chunks)
        def _():
            zi, zz, ch = turn(q)
            for cc in range(2):
                mine = jnp.logical_and(c + 2 * zz == z, c == cc)

                @pl.when(jnp.logical_not(mine))
                def _():
                    send(
                        wo_ref.at[:, pl.ds(0, CHUNK)],
                        wbuf.at[zz, y, cc, ch],
                        wl_s.at[0, 0],
                        wl_r.at[zz, cc, ch],
                        (d, mate),
                    ).wait_recv()

                forward(zz, cc, ch).start()
            block(zi, zz, y, ch)

        @pl.when(q > 0)
        def _():
            zi, zz, ch = turn(q - 1)
            for cc in range(2):
                forwarded(zz, cc, ch).wait_recv()
            block(zi, zz, 1 - y, ch)

        return 0

    lax.fori_loop(0, 2 * chunks + 1, stage, 0)

    dp_wait(9, lambda p: gsend.at[p], grecv)
    g = grecv[0]
    for i in range(1, ndp):
        g = g + grecv[i]
    ga_ref[...] = g[0]
    gb_ref[...] = g[1]
    for yy in range(2):
        for ch in range(chunks):
            share(yy, ch).wait_recv()
            cols = pl.ds((yy * chunks + ch) * CHUNK, CHUNK)
            out_ref[:, cols] += prcv[yy, ch]

    line_sends(False)
    for zz in range(2):
        for cc in range(2):
            for ch in range(chunks):
                forward(zz, cc, ch).wait_send()
    for yy in range(2):
        for ch in range(chunks):
            share(yy, ch).wait_send()

    @pl.when(bdst != d)
    def _():
        send(b_ref, bdbuf.at[bslot], bd_s.at[0], bd_r.at[bslot], (bdst, t)).wait_send()

    for cp in sent:
        cp.wait_send()


def fused_shards(
    ndp,
    ntp,
    hidden,
    attention_norm_gain,
    query_key_value_weight,
    key_value_cache,
    cache_fill_lengths,
    output_weight_frozen,
    adapter_down_transposed,
    adapter_up_matrix,
    attention_rows,
    upstream,
    rewards,
    prompt_group_index,
    completion_live_lengths,
):
    rolls, model = hidden.shape
    width = model // ndp
    rank, _, piece = adapter_down_transposed.shape
    rows, shard = attention_rows.shape
    qkvw = query_key_value_weight.shape[2]
    feats = output_weight_frozen.shape[1]
    chunks = width // CHUNK
    groups = rolls * ndp // GROUP
    h = hidden.astype(F32).reshape(rolls, ndp, width).transpose(1, 0, 2)
    gain = attention_norm_gain.astype(F32).reshape(ndp, 1, width)
    lane = jnp.arange(128, dtype=jnp.int32)
    onehot = (prompt_group_index[:, None] == lane[None, :]).astype(F32)
    spread = lambda v: jnp.broadcast_to(v.astype(F32)[:, None], (rolls, 128))
    stats = jnp.concatenate(
        [
            jnp.sum(onehot * rewards[:, None], axis=0, keepdims=True),
            jnp.sum(onehot * (rewards * rewards)[:, None], axis=0, keepdims=True),
            onehot,
            spread(rewards),
            spread(completion_live_lengths),
        ],
        axis=0,
    )
    vm = pl.BlockSpec(memory_space=pltpu.VMEM)
    sm = pl.BlockSpec(memory_space=pltpu.SMEM)
    dma = pltpu.SemaphoreType.DMA
    V = pltpu.VMEM
    dec, out, ga, gb = pl.pallas_call(
        lambda *refs: fused_kernel(ndp, ntp, *refs),
        out_shape=(
            jax.ShapeDtypeStruct((rolls, model), F32),
            jax.ShapeDtypeStruct((rows, shard), F32),
            jax.ShapeDtypeStruct((rank, piece), F32),
            jax.ShapeDtypeStruct((rank, piece), F32),
        ),
        in_specs=[vm, vm, vm, vm, sm, vm, vm, vm, vm, vm, vm],
        out_specs=(vm, vm, vm, vm),
        scratch_shapes=[
            V((ndp, rolls, width), F32),
            V((ndp, rank, piece), BF16),
            V((ndp, rank, piece), BF16),
            V((width // piece, rank, piece), BF16),
            V((ndp,) + stats.shape, F32),
            V((2, ndp, rolls, qkvw + 128), F32),
            V((2, ndp, rolls, qkvw + 128), F32),
            V((2, rolls, feats), F32),
            V((2, ndp, rolls, feats), F32),
            V((2, ndp * rolls, width + 128), F32),
            V((2, ntp, ndp * rolls, width + 128), F32),
            V((ndp, rolls, width), F32),
            V((ndp, rolls, width), F32),
            V((2, rank, rows), F32),
            V((ntp, 2, rank, rows), F32),
            V((ndp, 2, rank, piece), F32),
            V((ndp, 2, rank, piece), F32),
            V((rows, shard), BF16),
            V((2, rows, shard), BF16),
            V((2, 2, 2, chunks, feats, CHUNK), BF16),
            V((2, chunks, rows, CHUNK), F32),
            V((2, chunks, rows, CHUNK), F32),
            dma((10, ndp)),
            dma((10, ndp)),
            dma((3, ntp)),
            dma((3, ntp)),
            dma((ntp,)),
            dma((width // piece,)),
            dma((1,)),
            dma((1,)),
            dma((chunks, ndp // 2)),
            dma((2, 2, chunks)),
            dma((2, 2, chunks)),
            dma((2, 2, chunks)),
            dma((2, chunks)),
            dma((2, chunks)),
            dma((chunks,)),
        ],
        compiler_params=pltpu.CompilerParams(
            collective_id=0, has_side_effects=True, vmem_limit_bytes=60 * 2**20
        ),
    )(
        h,
        gain,
        query_key_value_weight[:, 0, :],
        key_value_cache[:, :, 0, :],
        cache_fill_lengths,
        output_weight_frozen[0],
        adapter_down_transposed[:, 0, :],
        adapter_up_matrix[:, 0, :],
        attention_rows,
        upstream,
        stats,
    )
    return dec, out, ga[:, None, :], gb[:, None, :]


def shards(
    hidden,
    attention_norm_gain,
    query_key_value_weight,
    key_value_cache,
    cache_fill_lengths,
    output_weight_frozen,
    adapter_down_transposed,
    adapter_up_matrix,
    attention_rows,
    upstream,
    rewards,
    prompt_group_index,
    completion_live_lengths,
):
    a_piece, b_piece = (
        lax.all_gather(adapter_down_transposed, "dp", axis=2, tiled=True),
        lax.all_gather(adapter_up_matrix, "dp", axis=2, tiled=True),
    )
    b_whole = lax.all_gather(b_piece, "tp", axis=1, tiled=True)
    up_matrix_flat = b_whole.reshape(b_whole.shape[0], -1).astype(jnp.float32)
    a_local = a_piece[:, 0, :]
    up_matrix_columns = b_piece[:, 0, :]
    w_rows = query_key_value_weight[:, 0, :].astype(jnp.float32)
    w_cols = output_weight_frozen[0]
    query_width = HEADS_TP * HD
    local_rolls = hidden.shape[0]
    decode_state = hidden.astype(jnp.float32)
    keys_new = []
    values_new = []
    for step in range(2):
        normed = rms_norm(decode_state, attention_norm_gain)
        spread = lax.all_to_all(normed, "dp", split_axis=1, concat_axis=0, tiled=True)
        partial_value = jnp.dot(spread, w_rows, precision=lax.Precision.HIGHEST)
        qkv = lax.psum_scatter(partial_value, "dp", scatter_dimension=0, tiled=True)
        query = qkv[:, :query_width].reshape(local_rolls, HEADS_TP, HD)
        keys_new.append(qkv[:, query_width : query_width + HD])
        values_new.append(qkv[:, query_width + HD :])
        attended = attend(
            query,
            key_value_cache[:, :, 0, :],
            cache_fill_lengths,
            jnp.stack(keys_new, axis=1),
            jnp.stack(values_new, axis=1),
        )
        columns = jnp.dot(
            lax.all_gather(attended, "dp", axis=0, tiled=True),
            w_cols,
            preferred_element_type=jnp.float32,
        )
        returned_values = lax.all_to_all(columns, "dp", split_axis=0, concat_axis=1, tiled=True)
        low_rank_decode = jnp.dot(attended, a_local.T, preferred_element_type=jnp.float32)
        state_update = returned_values + adapter_scale * jnp.dot(
            low_rank_decode, up_matrix_flat, precision=lax.Precision.HIGHEST
        )
        decode_state = decode_state + lax.psum(state_update, "tp")
    groups = local_rolls * lax.axis_size("dp") // GROUP
    onehot = (prompt_group_index[:, None] == jnp.arange(groups, dtype=jnp.int32)[None, :]).astype(
        jnp.float32
    )
    totals, squares = lax.psum(
        (
            jnp.sum(onehot * rewards[:, None], axis=0),
            jnp.sum(onehot * (rewards * rewards)[:, None], axis=0),
        ),
        "dp",
    )
    mean = totals / GROUP
    std = jnp.sqrt(jnp.maximum(squares / GROUP - mean * mean, 0.09))
    advantage = (rewards - jnp.sum(onehot * mean[None, :], axis=1)) / jnp.sum(
        onehot * std[None, :], axis=1
    )
    per_roll = advantage / completion_live_lengths.astype(jnp.float32)
    rows = attention_rows.shape[0]
    slot = jnp.arange(rows, dtype=jnp.int32) % COMP
    limit = jnp.repeat(completion_live_lengths, COMP)
    row_w = jnp.where(slot < limit, jnp.repeat(per_roll, COMP), 0.0)
    whole_rows = jnp.dot(
        attention_rows,
        lax.all_gather(output_weight_frozen, "dp", axis=2, tiled=True)[0],
        preferred_element_type=jnp.float32,
    )
    frozen_output_rows = lax.psum_scatter(whole_rows, "tp", scatter_dimension=1, tiled=True)
    low_sum = lax.psum(jnp.dot(attention_rows, a_local.T, preferred_element_type=jnp.float32), "tp")
    low_rank_rows = low_sum.astype(jnp.bfloat16)
    adapted_output_rows = frozen_output_rows + adapter_scale * jnp.dot(
        low_rank_rows, up_matrix_columns, preferred_element_type=jnp.float32
    )
    advantage_weighted = (row_w[:, None] * upstream.astype(jnp.float32)).astype(jnp.bfloat16)
    backward_result = lax.psum(
        jnp.dot(advantage_weighted, up_matrix_columns.T, preferred_element_type=jnp.float32), "tp"
    ).astype(jnp.bfloat16)
    down_gradient = adapter_scale * lax.dot_general(
        backward_result,
        attention_rows,
        (((0,), (0,)), ((), ())),
        preferred_element_type=jnp.float32,
    )
    up_gradient = adapter_scale * lax.dot_general(
        low_rank_rows,
        advantage_weighted,
        (((0,), (0,)), ((), ())),
        preferred_element_type=jnp.float32,
    )
    grad_a_part, grad_b_part = (
        lax.psum_scatter(down_gradient[:, None, :], "dp", scatter_dimension=2, tiled=True),
        lax.psum_scatter(up_gradient[:, None, :], "dp", scatter_dimension=2, tiled=True),
    )
    return (decode_state, adapted_output_rows, grad_a_part, grad_b_part)


def solution(mesh):
    placed = (
        P("dp", None),
        P(),
        P("dp", "tp", None),
        P("dp", None, "tp", None),
        P("dp"),
        P("tp", None, "dp"),
        P(None, "tp", "dp"),
        P(None, "tp", "dp"),
        P("dp", "tp"),
        P("dp", "tp"),
        P("dp"),
        P("dp"),
        P("dp"),
    )
    ndp, ntp = mesh.shape["dp"], mesh.shape["tp"]

    def body(*args):
        width = args[5].shape[2]
        piece = args[6].shape[2]
        if ntp == 4 and ndp == 8 and piece % 128 == 0 and width % CHUNK == 0:
            return fused_shards(ndp, ntp, *args)
        return shards(*args)

    return jax.shard_map(
        body,
        mesh=mesh,
        in_specs=placed,
        out_specs=(P("dp", None), P("dp", "tp"), P(None, "tp", "dp"), P(None, "tp", "dp")),
        check_vma=False,
    )
```

```python
import math

import jax
import jax.numpy as jnp
from jax import lax
from jax.experimental import pallas as pl
from jax.experimental.pallas import tpu as pltpu
from jax.sharding import PartitionSpec as P

HD = 128
HEADS_TP = 8
GROUP = 4
COMP = 256


adapter_scale = 2.0


def rms_norm(decode_state, gain):
    scale = lax.rsqrt(jnp.mean(decode_state * decode_state, axis=-1, keepdims=True) + 1e-05)
    return decode_state * scale * gain.astype(jnp.float32)


def attend(query, cache, lengths, new_keys, new_values):
    head = query.shape[-1]
    slots = cache.shape[1]
    factor = 1.0 / math.sqrt(head)
    keys = cache[:, :, :head].astype(jnp.float32)
    values = cache[:, :, head:]
    scores = jnp.einsum("bhd,bcd->bhc", query, keys, precision=lax.Precision.HIGHEST) * factor
    valid = jnp.arange(slots, dtype=jnp.int32)[None, None, :] < lengths[:, None, None]
    scores = jnp.where(valid, scores, -1e30)
    extra = jnp.einsum("bhd,bed->bhe", query, new_keys, precision=lax.Precision.HIGHEST) * factor
    joined = jnp.concatenate([scores, extra], axis=-1)
    top = jnp.max(joined, axis=-1, keepdims=True)
    expo = jnp.exp(joined - top)
    probs = (expo / jnp.sum(expo, axis=-1, keepdims=True)).astype(jnp.bfloat16)
    out = jnp.einsum("bhc,bcd->bhd", probs[..., :slots], values, preferred_element_type=jnp.float32)
    out = out + jnp.einsum(
        "bhe,bed->bhd",
        probs[..., slots:].astype(jnp.float32),
        new_values,
        precision=lax.Precision.HIGHEST,
    )
    return out.astype(jnp.bfloat16).reshape(query.shape[0], -1)


MESH = pl.DeviceIdType.MESH
F32 = jnp.float32
BF16 = jnp.bfloat16
NT = (((1,), (1,)), ((), ()))
TN = (((0,), (0,)), ((), ()))
CHUNK = 256
LINE_PARTS = 8
ROW_PARTS = 8


def split3(v):
    hi = v.astype(BF16)
    rest = v - hi.astype(F32)
    mid = rest.astype(BF16)
    lo = (rest - mid.astype(F32)).astype(BF16)
    return jnp.concatenate([hi, mid, lo], axis=0)


def exact_dot(v, w, dims=(((1,), (0,)), ((), ()))):
    n = v.shape[0]
    r = lax.dot_general(split3(v), w, dims, preferred_element_type=F32)
    return r[:n] + r[n : 2 * n] + r[2 * n :]


def rows_of(ref, n):
    return jnp.concatenate([ref[i] for i in range(n)], axis=0)


def lanes_of(ref, n):
    return jnp.concatenate([ref[i] for i in range(n)], axis=1)


def fused_kernel(
    ndp,
    ntp,
    h_ref,
    gain_ref,
    wqkv_ref,
    cache_ref,
    lens_ref,
    wo_ref,
    a_ref,
    b_ref,
    x_ref,
    up_ref,
    rew_ref,
    idx_ref,
    live_ref,
    dec_ref,
    out_ref,
    ga_ref,
    gb_ref,
    hsend,
    stats_ref,
    hbuf,
    abuf,
    bbuf,
    bdbuf,
    statbuf,
    qsend,
    qrecv,
    asend,
    arecv,
    usend,
    urecv,
    fsend,
    frecv,
    lbsend,
    lbrecv,
    gsend,
    grecv,
    wt_ref,
    xbuf,
    wbuf,
    pbuf,
    prcv,
    ds_s,
    ds_r,
    ts_s,
    ts_r,
    bd_s,
    bd_r,
    xs_s,
    xs_r,
    wl_s,
    wl_r,
    ps_s,
    ps_r,
):
    d = lax.axis_index("dp")
    t = lax.axis_index("tp")
    z, y = d // 2, d % 2
    x, c = t // 2, t % 2
    nz = ndp // 2
    rolls, model = h_ref.shape
    width = model // ndp
    rank = a_ref.shape[0]
    piece = a_ref.shape[1]
    chunks = wo_ref.shape[1] // CHUNK
    qkvw = wqkv_ref.shape[1]
    rows = x_ref.shape[0]

    barrier = pltpu.get_barrier_semaphore()
    for i in range(ndp):
        for j in range(ntp):
            if i or j:
                pl.semaphore_signal(
                    barrier,
                    inc=1,
                    device_id=((d + i) % ndp, (t + j) % ntp),
                    device_id_type=MESH,
                )
    pl.semaphore_wait(barrier, ndp * ntp - 1)

    sent = []

    def send(src, dst, s, r, dev):
        cp = pltpu.make_async_remote_copy(
            src_ref=src, dst_ref=dst, send_sem=s, recv_sem=r, device_id=dev, device_id_type=MESH
        )
        return cp

    def dp_start(e, src, dst):
        for off in range(1, ndp):
            peer = (d + off) % ndp
            cp = send(src(peer), dst.at[d], ds_s.at[e, off], ds_r.at[e, off], (peer, t))
            cp.start()
            sent.append(cp)

    def dp_wait(e, src, dst):
        for off in range(1, ndp):
            frm = (d + ndp - off) % ndp
            send(src(d), dst.at[frm], ds_s.at[e, off], ds_r.at[e, off], (frm, t)).wait_recv()

    def tp_start(e, src, dst):
        for off in range(1, ntp):
            peer = (t + off) % ntp
            cp = send(src, dst.at[t], ts_s.at[e, off], ts_r.at[e, off], (d, peer))
            cp.start()
            sent.append(cp)

    def tp_wait(e, src, dst):
        for off in range(1, ntp):
            frm = (t + ntp - off) % ntp
            send(src, dst.at[frm], ts_s.at[e, off], ts_r.at[e, off], (d, frm)).wait_recv()

    hidden = h_ref[...].astype(F32)
    for i in range(ndp):
        hsend[i] = hidden[:, i * width : (i + 1) * width]
    lane = lax.broadcasted_iota(jnp.int32, (1, 128), 1)
    ones = [jnp.where(lane == idx_ref[r], 1.0, 0.0) for r in range(rolls)]
    stats_ref[...] = jnp.zeros_like(stats_ref)
    for r in range(rolls):
        stats_ref[0:1] += ones[r] * rew_ref[r]
        stats_ref[1:2] += ones[r] * (rew_ref[r] * rew_ref[r])

    dp_start(0, lambda p: hsend.at[p], hbuf)
    hbuf[d] = hsend[d]
    dp_start(1, lambda p: a_ref, abuf)
    abuf[d] = a_ref[...]
    dp_start(2, lambda p: b_ref, bbuf)
    bbuf[d] = b_ref[...]
    dp_start(3, lambda p: stats_ref, statbuf)
    statbuf[d] = stats_ref[...]
    per = width // piece
    half = ndp // per
    bdst = t * half + d // per
    bslot = d % per
    for j in range(ntp):
        tj = (t + j) % ntp
        if j == 0:
            here = bdst == d

            @pl.when(here)
            def _():
                bdbuf[bslot] = b_ref[...]

            @pl.when(jnp.logical_not(here))
            def _():
                send(b_ref, bdbuf.at[bslot], bd_s.at[0], bd_r.at[bslot], (bdst, tj)).start()

        else:
            cp = send(b_ref, bdbuf.at[bslot], bd_s.at[j], bd_r.at[bslot], (bdst, tj))
            cp.start()
            sent.append(cp)
    mate = 2 * x + (1 - c)
    other_y = 2 * z + (1 - y)
    xcp = send(x_ref, xbuf.at[y, c], xs_s.at[0], xs_r.at[0], (d, mate))
    xcp.start()
    sent.append(xcp)
    xbuf[y, c] = x_ref[...]

    def row_send(k):
        part = rows // ROW_PARTS
        seg = pl.ds(k * part, part)
        send(
            x_ref.at[seg], xbuf.at[y, c, seg], xs_s.at[1], xs_r.at[1], (other_y, t)
        ).start()

    def rows_whole():
        return send(x_ref, xbuf.at[1 - y, c], xs_s.at[1], xs_r.at[1], (other_y, t))

    def relay(dst_core):
        return send(
            xbuf.at[1 - y, c], xbuf.at[1 - y, dst_core], xs_s.at[2], xs_r.at[2], (d, mate)
        )

    def line(ch, off, seg):
        zt = (z + off) % nz
        cols = pl.ds(ch * CHUNK, CHUNK)
        return send(
            wo_ref.at[seg, cols],
            wbuf.at[z // 2, c, ch, seg],
            wl_s.at[ch, off],
            wl_r.at[z // 2, c, ch],
            (2 * zt + y, 2 * x + z % 2),
        )

    def quantum(k):
        ch, part = k // LINE_PARTS, k % LINE_PARTS
        size = wo_ref.shape[0] // LINE_PARTS
        seg = pl.ds(part * size, size)
        for off in (1, 3, 2):
            line(ch, off, seg).start()

        @pl.when(z % 2 != c)
        def _():
            line(ch, 0, seg).start()

    pending = list(range(chunks * LINE_PARTS))
    row_parts = list(range(ROW_PARTS))

    def bulk(n, m=0):
        for _ in range(min(n, len(pending))):
            quantum(pending.pop(0))
        for _ in range(min(m, len(row_parts))):
            row_send(row_parts.pop(0))

    bulk(1, 1)

    @pl.when(z % 2 == c)
    def _():
        for ch in range(chunks):
            wbuf[z // 2, c, ch] = wo_ref[:, ch * CHUNK : (ch + 1) * CHUNK]

    dp_wait(0, lambda p: hsend.at[p], hbuf)
    state = rows_of(hbuf, ndp)
    gain = gain_ref[:, pl.ds(pl.multiple_of(d * width, width), width)].astype(F32)
    new_k, new_v = [], []
    factor = 1.0 / math.sqrt(HD)

    for step in range(2):
        squares = jnp.sum(state * state, axis=-1, keepdims=True)
        part = exact_dot(state * gain, wqkv_ref[...])
        both = jnp.concatenate([part, jnp.broadcast_to(squares, (ndp * rolls, 128))], axis=1)
        for i in range(ndp):
            qsend[step, i] = both[i * rolls : (i + 1) * rolls]
        dp_start(4 + 2 * step, lambda p: qsend.at[step, p], qrecv.at[step])
        bulk(2, 2)
        qrecv[step, d] = qsend[step, d]
        if step == 0:
            dp_wait(1, lambda p: a_ref, abuf)
            at = lanes_of(abuf, ndp)
            dp_wait(2, lambda p: b_ref, bbuf)
            bt = lanes_of(bbuf, ndp)
            dp_wait(3, lambda p: stats_ref, statbuf)
            tot = statbuf[0]
            for i in range(1, ndp):
                tot = tot + statbuf[i]
            mean = tot[0:1] / GROUP
            std = jnp.sqrt(jnp.maximum(tot[1:2] / GROUP - mean * mean, 0.09))
            for r in range(rolls):
                one, rew = ones[r], rew_ref[r]
                live = live_ref[r].astype(F32)
                adv = (rew - jnp.sum(one * mean, axis=1, keepdims=True)) / jnp.sum(
                    one * std, axis=1, keepdims=True
                )
                slot = lax.broadcasted_iota(jnp.int32, (COMP, 1), 0).astype(F32)
                row_w = jnp.where(slot < live, adv / live, 0.0)
                seg = pl.ds(r * COMP, COMP)
                wt_ref[seg, :] = (row_w * up_ref[seg, :].astype(F32)).astype(BF16)
            lbsend[0] = lax.dot_general(at, x_ref[...], NT, preferred_element_type=F32)
            lbsend[1] = lax.dot_general(bt, wt_ref[...], NT, preferred_element_type=F32)
        dp_wait(4 + 2 * step, lambda p: qsend.at[step, p], qrecv.at[step])
        total = qrecv[step, 0]
        for i in range(1, ndp):
            total = total + qrecv[step, i]
        qkv = total[:, :qkvw] * lax.rsqrt(total[:, qkvw : qkvw + 1] / model + 1e-05)
        new_k.append(qkv[:, HEADS_TP * HD : HEADS_TP * HD + HD])
        new_v.append(qkv[:, HEADS_TP * HD + HD :])
        for b in range(rolls):
            q = jnp.concatenate(
                [qkv[b : b + 1, h * HD : (h + 1) * HD] for h in range(HEADS_TP)], axis=0
            )
            scores = exact_dot(q, cache_ref[b, :, :HD], NT) * factor
            pos = lax.broadcasted_iota(jnp.int32, scores.shape, 1)
            scores = jnp.where(pos < lens_ref[b], scores, -1e30)
            extra = [
                jnp.sum(q * k[b : b + 1], axis=-1, keepdims=True) * factor for k in new_k
            ]
            top = jnp.max(scores, axis=-1, keepdims=True)
            for e in extra:
                top = jnp.maximum(top, e)
            expo = jnp.exp(scores - top)
            ee = [jnp.exp(e - top) for e in extra]
            den = jnp.sum(expo, axis=-1, keepdims=True)
            for e in ee:
                den = den + e
            att = jnp.dot(
                (expo / den).astype(BF16), cache_ref[b, :, HD:], preferred_element_type=F32
            )
            for e, v in zip(ee, new_v):
                att = att + (e / den).astype(BF16).astype(F32) * v[b : b + 1]
            att = att.astype(BF16).astype(F32)
            asend[step, b : b + 1, :] = jnp.concatenate(
                [att[h : h + 1] for h in range(HEADS_TP)], axis=1
            )
        dp_start(5 + 2 * step, lambda p: asend.at[step], arecv.at[step])
        bulk(1, 1)
        arecv[step, d] = asend[step]
        if step == 0:
            tp_start(2, lbsend, lbrecv)
            lbrecv[t] = lbsend[...]
        else:
            tp_wait(2, lbsend, lbrecv)
            lb = lbrecv[0]
            for i in range(1, ntp):
                lb = lb + lbrecv[i]
            lb = lb.astype(BF16)
            low_t, back_t = lb[0], lb[1]
            ga = adapter_scale * jnp.dot(back_t, x_ref[...], preferred_element_type=F32)
            gb = adapter_scale * jnp.dot(low_t, wt_ref[...], preferred_element_type=F32)
            for i in range(ndp):
                gsend[i, 0] = ga[:, i * piece : (i + 1) * piece]
                gsend[i, 1] = gb[:, i * piece : (i + 1) * piece]
        dp_wait(5 + 2 * step, lambda p: asend.at[step], arecv.at[step])
        attended = rows_of(arecv.at[step], ndp).astype(BF16)
        usend[step, :, :width] = jnp.dot(attended, wo_ref[...], preferred_element_type=F32)
        usend[step, :, width:] = jnp.concatenate(
            [
                lax.dot_general(attended, at, NT, preferred_element_type=F32),
                jnp.zeros((ndp * rolls, 128 - rank), F32),
            ],
            axis=1,
        )
        tp_start(step, usend.at[step], urecv.at[step])
        bulk(1, 1)
        urecv[step, t] = usend[step]
        if step == 0:
            src_t = d // half
            for j in range(per):
                frm = (d % half) * per + j
                same = jnp.logical_and(src_t == t, frm == d)

                @pl.when(jnp.logical_not(same))
                def _():
                    send(b_ref, bdbuf.at[j], bd_s.at[0], bd_r.at[j], (frm, src_t)).wait_recv()

            bd = lanes_of(bdbuf, per)
        tp_wait(step, usend.at[step], urecv.at[step])
        upd = urecv[step, 0]
        for i in range(1, ntp):
            upd = upd + urecv[step, i]
        state = state + (
            upd[:, :width] + adapter_scale * exact_dot(upd[:, width : width + rank], bd)
        )

    for i in range(ndp):
        fsend[i] = state[i * rolls : (i + 1) * rolls]
    dp_start(8, lambda p: fsend.at[p], frecv)
    frecv[d] = fsend[d]
    dp_start(9, lambda p: gsend.at[p], grecv)
    grecv[d] = gsend[d]
    bulk(len(pending), len(row_parts))
    rows_whole().wait_recv()
    relay(c).start()
    out_ref[...] = adapter_scale * lax.dot_general(low_t, bt, TN, preferred_element_type=F32)
    send(x_ref, xbuf.at[y, 1 - c], xs_s.at[0], xs_r.at[0], (d, mate)).wait_recv()
    dp_wait(8, lambda p: fsend.at[p], frecv)
    for i in range(ndp):
        dec_ref[:, i * width : (i + 1) * width] = frecv[i]
    relay(1 - c).wait_recv()

    def share(dx, dy, ch):
        zz = jnp.where(dx == 1, 1 - x, x)
        yy = jnp.where(dy == 1, 1 - y, y)
        return send(
            pbuf.at[dx, dy, ch],
            prcv.at[dx, dy, ch],
            ps_s.at[dx, dy, ch],
            ps_r.at[dx, dy, ch],
            (2 * z + yy, 2 * zz + c),
        )

    def stage(q, _):
        ch, r = q // 4, q % 4
        dx, dy = 1 - r // 2, 1 - r % 2
        zz = jnp.where(dx == 1, 1 - x, x)
        yy = jnp.where(dy == 1, 1 - y, y)

        @pl.when(dy == 1)
        def _():
            for cc in range(2):
                mine = jnp.logical_and(c + 2 * zz == z, c == cc)

                @pl.when(jnp.logical_not(mine))
                def _():
                    send(
                        wo_ref.at[:, pl.ds(0, CHUNK)],
                        wbuf.at[zz, cc, ch],
                        wl_s.at[0, 0],
                        wl_r.at[zz, cc, ch],
                        (d, mate),
                    ).wait_recv()

        p = jnp.dot(xbuf[yy, 0], wbuf[zz, 0, ch], preferred_element_type=F32)
        p = p + jnp.dot(xbuf[yy, 1], wbuf[zz, 1, ch], preferred_element_type=F32)
        last = r == 3

        @pl.when(jnp.logical_not(last))
        def _():
            pbuf[dx, dy, ch] = p
            share(dx, dy, ch).start()

        @pl.when(last)
        def _():
            cols = pl.ds(pl.multiple_of((y * chunks + ch) * CHUNK, CHUNK), CHUNK)
            out_ref[:, cols] += p

        return 0

    lax.fori_loop(0, 4 * chunks, stage, 0)

    dp_wait(9, lambda p: gsend.at[p], grecv)
    g = grecv[0]
    for i in range(1, ndp):
        g = g + grecv[i]
    ga_ref[...] = g[0]
    gb_ref[...] = g[1]
    for ch in range(chunks):
        for dx, dy in ((1, 0), (0, 1), (1, 1)):
            share(dx, dy, ch).wait_recv()
            yy = (y + dy) % 2
            cols = pl.ds(pl.multiple_of((yy * chunks + ch) * CHUNK, CHUNK), CHUNK)
            out_ref[:, cols] += prcv[dx, dy, ch]

    whole = pl.ds(0, wo_ref.shape[0])
    for ch in range(chunks):
        for off in range(1, nz):
            line(ch, off, whole).wait_send()

        @pl.when(z % 2 != c)
        def _():
            line(ch, 0, whole).wait_send()

        for dx, dy in ((1, 0), (0, 1), (1, 1)):
            share(dx, dy, ch).wait_send()
    rows_whole().wait_send()
    relay(c).wait_send()

    @pl.when(bdst != d)
    def _():
        send(b_ref, bdbuf.at[bslot], bd_s.at[0], bd_r.at[bslot], (bdst, t)).wait_send()

    for cp in sent:
        cp.wait_send()


def fused_shards(
    ndp,
    ntp,
    hidden,
    attention_norm_gain,
    query_key_value_weight,
    key_value_cache,
    cache_fill_lengths,
    output_weight_frozen,
    adapter_down_transposed,
    adapter_up_matrix,
    attention_rows,
    upstream,
    rewards,
    prompt_group_index,
    completion_live_lengths,
):
    rolls, model = hidden.shape
    width = model // ndp
    rank, _, piece = adapter_down_transposed.shape
    rows, shard = attention_rows.shape
    qkvw = query_key_value_weight.shape[2]
    feats = output_weight_frozen.shape[1]
    chunks = width // CHUNK
    vm = pl.BlockSpec(memory_space=pltpu.VMEM)
    sm = pl.BlockSpec(memory_space=pltpu.SMEM)
    dma = pltpu.SemaphoreType.DMA
    V = pltpu.VMEM
    dec, out, ga, gb = pl.pallas_call(
        lambda *refs: fused_kernel(ndp, ntp, *refs),
        out_shape=(
            jax.ShapeDtypeStruct((rolls, model), F32),
            jax.ShapeDtypeStruct((rows, shard), F32),
            jax.ShapeDtypeStruct((rank, piece), F32),
            jax.ShapeDtypeStruct((rank, piece), F32),
        ),
        in_specs=[vm, vm, vm, vm, sm, vm, vm, vm, vm, vm, sm, sm, sm],
        out_specs=(vm, vm, vm, vm),
        scratch_shapes=[
            V((ndp, rolls, width), F32),
            V((8, 128), F32),
            V((ndp, rolls, width), F32),
            V((ndp, rank, piece), BF16),
            V((ndp, rank, piece), BF16),
            V((width // piece, rank, piece), BF16),
            V((ndp, 8, 128), F32),
            V((2, ndp, rolls, qkvw + 128), F32),
            V((2, ndp, rolls, qkvw + 128), F32),
            V((2, rolls, feats), F32),
            V((2, ndp, rolls, feats), F32),
            V((2, ndp * rolls, width + 128), F32),
            V((2, ntp, ndp * rolls, width + 128), F32),
            V((ndp, rolls, width), F32),
            V((ndp, rolls, width), F32),
            V((2, rank, rows), F32),
            V((ntp, 2, rank, rows), F32),
            V((ndp, 2, rank, piece), F32),
            V((ndp, 2, rank, piece), F32),
            V((rows, shard), BF16),
            V((2, 2, rows, shard), BF16),
            V((2, 2, chunks, feats, CHUNK), BF16),
            V((2, 2, chunks, rows, CHUNK), F32),
            V((2, 2, chunks, rows, CHUNK), F32),
            dma((10, ndp)),
            dma((10, ndp)),
            dma((3, ntp)),
            dma((3, ntp)),
            dma((ntp,)),
            dma((width // piece,)),
            dma((3,)),
            dma((3,)),
            dma((chunks, ndp // 2)),
            dma((2, 2, chunks)),
            dma((2, 2, chunks)),
            dma((2, 2, chunks)),
        ],
        compiler_params=pltpu.CompilerParams(
            collective_id=0, has_side_effects=True, vmem_limit_bytes=60 * 2**20
        ),
    )(
        hidden,
        attention_norm_gain.reshape(1, model),
        query_key_value_weight[:, 0, :],
        key_value_cache[:, :, 0, :],
        cache_fill_lengths,
        output_weight_frozen[0],
        adapter_down_transposed[:, 0, :],
        adapter_up_matrix[:, 0, :],
        attention_rows,
        upstream,
        rewards,
        prompt_group_index,
        completion_live_lengths,
    )
    return dec, out, ga[:, None, :], gb[:, None, :]


def shards(
    hidden,
    attention_norm_gain,
    query_key_value_weight,
    key_value_cache,
    cache_fill_lengths,
    output_weight_frozen,
    adapter_down_transposed,
    adapter_up_matrix,
    attention_rows,
    upstream,
    rewards,
    prompt_group_index,
    completion_live_lengths,
):
    a_piece, b_piece = (
        lax.all_gather(adapter_down_transposed, "dp", axis=2, tiled=True),
        lax.all_gather(adapter_up_matrix, "dp", axis=2, tiled=True),
    )
    b_whole = lax.all_gather(b_piece, "tp", axis=1, tiled=True)
    up_matrix_flat = b_whole.reshape(b_whole.shape[0], -1).astype(jnp.float32)
    a_local = a_piece[:, 0, :]
    up_matrix_columns = b_piece[:, 0, :]
    w_rows = query_key_value_weight[:, 0, :].astype(jnp.float32)
    w_cols = output_weight_frozen[0]
    query_width = HEADS_TP * HD
    local_rolls = hidden.shape[0]
    decode_state = hidden.astype(jnp.float32)
    keys_new = []
    values_new = []
    for step in range(2):
        normed = rms_norm(decode_state, attention_norm_gain)
        spread = lax.all_to_all(normed, "dp", split_axis=1, concat_axis=0, tiled=True)
        partial_value = jnp.dot(spread, w_rows, precision=lax.Precision.HIGHEST)
        qkv = lax.psum_scatter(partial_value, "dp", scatter_dimension=0, tiled=True)
        query = qkv[:, :query_width].reshape(local_rolls, HEADS_TP, HD)
        keys_new.append(qkv[:, query_width : query_width + HD])
        values_new.append(qkv[:, query_width + HD :])
        attended = attend(
            query,
            key_value_cache[:, :, 0, :],
            cache_fill_lengths,
            jnp.stack(keys_new, axis=1),
            jnp.stack(values_new, axis=1),
        )
        columns = jnp.dot(
            lax.all_gather(attended, "dp", axis=0, tiled=True),
            w_cols,
            preferred_element_type=jnp.float32,
        )
        returned_values = lax.all_to_all(columns, "dp", split_axis=0, concat_axis=1, tiled=True)
        low_rank_decode = jnp.dot(attended, a_local.T, preferred_element_type=jnp.float32)
        state_update = returned_values + adapter_scale * jnp.dot(
            low_rank_decode, up_matrix_flat, precision=lax.Precision.HIGHEST
        )
        decode_state = decode_state + lax.psum(state_update, "tp")
    groups = local_rolls * lax.axis_size("dp") // GROUP
    onehot = (prompt_group_index[:, None] == jnp.arange(groups, dtype=jnp.int32)[None, :]).astype(
        jnp.float32
    )
    totals, squares = lax.psum(
        (
            jnp.sum(onehot * rewards[:, None], axis=0),
            jnp.sum(onehot * (rewards * rewards)[:, None], axis=0),
        ),
        "dp",
    )
    mean = totals / GROUP
    std = jnp.sqrt(jnp.maximum(squares / GROUP - mean * mean, 0.09))
    advantage = (rewards - jnp.sum(onehot * mean[None, :], axis=1)) / jnp.sum(
        onehot * std[None, :], axis=1
    )
    per_roll = advantage / completion_live_lengths.astype(jnp.float32)
    rows = attention_rows.shape[0]
    slot = jnp.arange(rows, dtype=jnp.int32) % COMP
    limit = jnp.repeat(completion_live_lengths, COMP)
    row_w = jnp.where(slot < limit, jnp.repeat(per_roll, COMP), 0.0)
    whole_rows = jnp.dot(
        attention_rows,
        lax.all_gather(output_weight_frozen, "dp", axis=2, tiled=True)[0],
        preferred_element_type=jnp.float32,
    )
    frozen_output_rows = lax.psum_scatter(whole_rows, "tp", scatter_dimension=1, tiled=True)
    low_sum = lax.psum(jnp.dot(attention_rows, a_local.T, preferred_element_type=jnp.float32), "tp")
    low_rank_rows = low_sum.astype(jnp.bfloat16)
    adapted_output_rows = frozen_output_rows + adapter_scale * jnp.dot(
        low_rank_rows, up_matrix_columns, preferred_element_type=jnp.float32
    )
    advantage_weighted = (row_w[:, None] * upstream.astype(jnp.float32)).astype(jnp.bfloat16)
    backward_result = lax.psum(
        jnp.dot(advantage_weighted, up_matrix_columns.T, preferred_element_type=jnp.float32), "tp"
    ).astype(jnp.bfloat16)
    down_gradient = adapter_scale * lax.dot_general(
        backward_result,
        attention_rows,
        (((0,), (0,)), ((), ())),
        preferred_element_type=jnp.float32,
    )
    up_gradient = adapter_scale * lax.dot_general(
        low_rank_rows,
        advantage_weighted,
        (((0,), (0,)), ((), ())),
        preferred_element_type=jnp.float32,
    )
    grad_a_part, grad_b_part = (
        lax.psum_scatter(down_gradient[:, None, :], "dp", scatter_dimension=2, tiled=True),
        lax.psum_scatter(up_gradient[:, None, :], "dp", scatter_dimension=2, tiled=True),
    )
    return (decode_state, adapted_output_rows, grad_a_part, grad_b_part)


def solution(mesh):
    placed = (
        P("dp", None),
        P(),
        P("dp", "tp", None),
        P("dp", None, "tp", None),
        P("dp"),
        P("tp", None, "dp"),
        P(None, "tp", "dp"),
        P(None, "tp", "dp"),
        P("dp", "tp"),
        P("dp", "tp"),
        P("dp"),
        P("dp"),
        P("dp"),
    )
    ndp, ntp = mesh.shape["dp"], mesh.shape["tp"]

    def body(*args):
        width = args[5].shape[2]
        piece = args[6].shape[2]
        if ntp == 4 and ndp == 8 and piece % 128 == 0 and width % CHUNK == 0:
            return fused_shards(ndp, ntp, *args)
        return shards(*args)

    return jax.shard_map(
        body,
        mesh=mesh,
        in_specs=placed,
        out_specs=(P("dp", None), P("dp", "tp"), P(None, "tp", "dp"), P(None, "tp", "dp")),
        check_vma=False,
    )
```

```python
import math

import jax
import jax.numpy as jnp
from jax import lax
from jax.experimental import pallas as pl
from jax.experimental.pallas import tpu as pltpu
from jax.sharding import PartitionSpec as P

HD = 128
HEADS_TP = 8
GROUP = 4
COMP = 256


adapter_scale = 2.0


def rms_norm(decode_state, gain):
    scale = lax.rsqrt(jnp.mean(decode_state * decode_state, axis=-1, keepdims=True) + 1e-05)
    return decode_state * scale * gain.astype(jnp.float32)


def attend(query, cache, lengths, new_keys, new_values):
    head = query.shape[-1]
    slots = cache.shape[1]
    factor = 1.0 / math.sqrt(head)
    keys = cache[:, :, :head].astype(jnp.float32)
    values = cache[:, :, head:]
    scores = jnp.einsum("bhd,bcd->bhc", query, keys, precision=lax.Precision.HIGHEST) * factor
    valid = jnp.arange(slots, dtype=jnp.int32)[None, None, :] < lengths[:, None, None]
    scores = jnp.where(valid, scores, -1e30)
    extra = jnp.einsum("bhd,bed->bhe", query, new_keys, precision=lax.Precision.HIGHEST) * factor
    joined = jnp.concatenate([scores, extra], axis=-1)
    top = jnp.max(joined, axis=-1, keepdims=True)
    expo = jnp.exp(joined - top)
    probs = (expo / jnp.sum(expo, axis=-1, keepdims=True)).astype(jnp.bfloat16)
    out = jnp.einsum("bhc,bcd->bhd", probs[..., :slots], values, preferred_element_type=jnp.float32)
    out = out + jnp.einsum(
        "bhe,bed->bhd",
        probs[..., slots:].astype(jnp.float32),
        new_values,
        precision=lax.Precision.HIGHEST,
    )
    return out.astype(jnp.bfloat16).reshape(query.shape[0], -1)


MESH = pl.DeviceIdType.MESH
F32 = jnp.float32
BF16 = jnp.bfloat16
NT = (((1,), (1,)), ((), ()))
TN = (((0,), (0,)), ((), ()))
CHUNK = 256
LINE_PARTS = 8
ROW_PARTS = 8


def split3(v):
    hi = v.astype(BF16)
    rest = v - hi.astype(F32)
    mid = rest.astype(BF16)
    lo = (rest - mid.astype(F32)).astype(BF16)
    return jnp.concatenate([hi, mid, lo], axis=0)


def exact_dot(v, w, dims=(((1,), (0,)), ((), ()))):
    n = v.shape[0]
    r = lax.dot_general(split3(v), w, dims, preferred_element_type=F32)
    return r[:n] + r[n : 2 * n] + r[2 * n :]


def rows_of(ref, n):
    return jnp.concatenate([ref[i] for i in range(n)], axis=0)


def lanes_of(ref, n):
    return jnp.concatenate([ref[i] for i in range(n)], axis=1)


def fused_kernel(
    ndp,
    ntp,
    h_ref,
    gain_ref,
    wqkv_ref,
    cache_ref,
    lens_ref,
    wo_ref,
    a_ref,
    b_ref,
    x_ref,
    up_ref,
    rew_ref,
    idx_ref,
    live_ref,
    dec_ref,
    out_ref,
    ga_ref,
    gb_ref,
    hsend,
    stats_ref,
    hbuf,
    abuf,
    bbuf,
    bdbuf,
    statbuf,
    qsend,
    qrecv,
    asend,
    arecv,
    usend,
    urecv,
    fsend,
    frecv,
    lbsend,
    lbrecv,
    gsend,
    grecv,
    wt_ref,
    xbuf,
    wbuf,
    pbuf,
    prcv,
    ds_s,
    ds_r,
    ts_s,
    ts_r,
    bd_s,
    bd_r,
    xs_s,
    xs_r,
    wl_s,
    wl_r,
    ps_s,
    ps_r,
):
    d = lax.axis_index("dp")
    t = lax.axis_index("tp")
    z, y = d // 2, d % 2
    x, c = t // 2, t % 2
    nz = ndp // 2
    rolls, model = h_ref.shape
    width = model // ndp
    rank = a_ref.shape[0]
    piece = a_ref.shape[1]
    chunks = wo_ref.shape[1] // CHUNK
    qkvw = wqkv_ref.shape[1]
    rows = x_ref.shape[0]

    barrier = pltpu.get_barrier_semaphore()
    for i in range(ndp):
        for j in range(ntp):
            if i or j:
                pl.semaphore_signal(
                    barrier,
                    inc=1,
                    device_id=((d + i) % ndp, (t + j) % ntp),
                    device_id_type=MESH,
                )
    pl.semaphore_wait(barrier, ndp * ntp - 1)

    sent = []

    def send(src, dst, s, r, dev):
        cp = pltpu.make_async_remote_copy(
            src_ref=src, dst_ref=dst, send_sem=s, recv_sem=r, device_id=dev, device_id_type=MESH
        )
        return cp

    def dp_start(e, src, dst):
        for off in range(1, ndp):
            peer = (d + off) % ndp
            cp = send(src(peer), dst.at[d], ds_s.at[e, off], ds_r.at[e, off], (peer, t))
            cp.start()
            sent.append(cp)

    def dp_wait(e, src, dst):
        for off in range(1, ndp):
            frm = (d + ndp - off) % ndp
            send(src(d), dst.at[frm], ds_s.at[e, off], ds_r.at[e, off], (frm, t)).wait_recv()

    def tp_start(e, src, dst):
        for off in range(1, ntp):
            peer = (t + off) % ntp
            cp = send(src, dst.at[t], ts_s.at[e, off], ts_r.at[e, off], (d, peer))
            cp.start()
            sent.append(cp)

    def tp_wait(e, src, dst):
        for off in range(1, ntp):
            frm = (t + ntp - off) % ntp
            send(src, dst.at[frm], ts_s.at[e, off], ts_r.at[e, off], (d, frm)).wait_recv()

    hidden = h_ref[...].astype(F32)
    for i in range(ndp):
        hsend[i] = hidden[:, i * width : (i + 1) * width]
    lane = lax.broadcasted_iota(jnp.int32, (1, 128), 1)
    ones = [jnp.where(lane == idx_ref[r], 1.0, 0.0) for r in range(rolls)]
    stats_ref[...] = jnp.zeros_like(stats_ref)
    for r in range(rolls):
        stats_ref[0:1] += ones[r] * rew_ref[r]
        stats_ref[1:2] += ones[r] * (rew_ref[r] * rew_ref[r])

    dp_start(0, lambda p: hsend.at[p], hbuf)
    hbuf[d] = hsend[d]
    dp_start(1, lambda p: a_ref, abuf)
    abuf[d] = a_ref[...]
    dp_start(2, lambda p: b_ref, bbuf)
    bbuf[d] = b_ref[...]
    dp_start(3, lambda p: stats_ref, statbuf)
    statbuf[d] = stats_ref[...]
    per = width // piece
    half = ndp // per
    bdst = t * half + d // per
    bslot = d % per
    for j in range(ntp):
        tj = (t + j) % ntp
        if j == 0:
            here = bdst == d

            @pl.when(here)
            def _():
                bdbuf[bslot] = b_ref[...]

            @pl.when(jnp.logical_not(here))
            def _():
                send(b_ref, bdbuf.at[bslot], bd_s.at[0], bd_r.at[bslot], (bdst, tj)).start()

        else:
            cp = send(b_ref, bdbuf.at[bslot], bd_s.at[j], bd_r.at[bslot], (bdst, tj))
            cp.start()
            sent.append(cp)
    mate = 2 * x + (1 - c)
    other_y = 2 * z + (1 - y)
    xcp = send(x_ref, xbuf.at[y, c], xs_s.at[0], xs_r.at[0], (d, mate))
    xcp.start()
    sent.append(xcp)
    xbuf[y, c] = x_ref[...]

    def row_send(k):
        part = rows // ROW_PARTS
        seg = pl.ds(k * part, part)
        send(
            x_ref.at[seg], xbuf.at[y, c, seg], xs_s.at[1], xs_r.at[1], (other_y, t)
        ).start()

    def rows_whole():
        return send(x_ref, xbuf.at[1 - y, c], xs_s.at[1], xs_r.at[1], (other_y, t))

    def relay(dst_core):
        return send(
            xbuf.at[1 - y, c], xbuf.at[1 - y, dst_core], xs_s.at[2], xs_r.at[2], (d, mate)
        )

    def line(ch, off, seg):
        zt = (z + off) % nz
        cols = pl.ds(ch * CHUNK, CHUNK)
        return send(
            wo_ref.at[seg, cols],
            wbuf.at[z // 2, c, ch, seg],
            wl_s.at[ch, off],
            wl_r.at[z // 2, c, ch],
            (2 * zt + y, 2 * x + z % 2),
        )

    def quantum(k):
        ch, part = k // LINE_PARTS, k % LINE_PARTS
        size = wo_ref.shape[0] // LINE_PARTS
        seg = pl.ds(part * size, size)
        for off in (1, 3, 2):
            line(ch, off, seg).start()

        @pl.when(z % 2 != c)
        def _():
            line(ch, 0, seg).start()

    pending = list(range(chunks * LINE_PARTS))
    row_parts = list(range(ROW_PARTS))

    def bulk(n, m=0):
        for _ in range(min(n, len(pending))):
            quantum(pending.pop(0))
        for _ in range(min(m, len(row_parts))):
            row_send(row_parts.pop(0))

    bulk(1, 1)

    @pl.when(z % 2 == c)
    def _():
        for ch in range(chunks):
            wbuf[z // 2, c, ch] = wo_ref[:, ch * CHUNK : (ch + 1) * CHUNK]

    dp_wait(0, lambda p: hsend.at[p], hbuf)
    state = rows_of(hbuf, ndp)
    gain = gain_ref[:, pl.ds(pl.multiple_of(d * width, width), width)].astype(F32)
    new_k, new_v = [], []
    factor = 1.0 / math.sqrt(HD)

    for step in range(2):
        squares = jnp.sum(state * state, axis=-1, keepdims=True)
        part = exact_dot(state * gain, wqkv_ref[...])
        both = jnp.concatenate([part, jnp.broadcast_to(squares, (ndp * rolls, 128))], axis=1)
        for i in range(ndp):
            qsend[step, i] = both[i * rolls : (i + 1) * rolls]
        dp_start(4 + 2 * step, lambda p: qsend.at[step, p], qrecv.at[step])
        bulk(1, 2)
        qrecv[step, d] = qsend[step, d]
        if step == 0:
            dp_wait(1, lambda p: a_ref, abuf)
            at = lanes_of(abuf, ndp)
            dp_wait(2, lambda p: b_ref, bbuf)
            bt = lanes_of(bbuf, ndp)
            dp_wait(3, lambda p: stats_ref, statbuf)
            tot = statbuf[0]
            for i in range(1, ndp):
                tot = tot + statbuf[i]
            mean = tot[0:1] / GROUP
            std = jnp.sqrt(jnp.maximum(tot[1:2] / GROUP - mean * mean, 0.09))
            for r in range(rolls):
                one, rew = ones[r], rew_ref[r]
                live = live_ref[r].astype(F32)
                adv = (rew - jnp.sum(one * mean, axis=1, keepdims=True)) / jnp.sum(
                    one * std, axis=1, keepdims=True
                )
                slot = lax.broadcasted_iota(jnp.int32, (COMP, 1), 0).astype(F32)
                row_w = jnp.where(slot < live, adv / live, 0.0)
                seg = pl.ds(r * COMP, COMP)
                wt_ref[seg, :] = (row_w * up_ref[seg, :].astype(F32)).astype(BF16)
            lbsend[0] = lax.dot_general(at, x_ref[...], NT, preferred_element_type=F32)
            lbsend[1] = lax.dot_general(bt, wt_ref[...], NT, preferred_element_type=F32)
        dp_wait(4 + 2 * step, lambda p: qsend.at[step, p], qrecv.at[step])
        total = qrecv[step, 0]
        for i in range(1, ndp):
            total = total + qrecv[step, i]
        qkv = total[:, :qkvw] * lax.rsqrt(total[:, qkvw : qkvw + 1] / model + 1e-05)
        new_k.append(qkv[:, HEADS_TP * HD : HEADS_TP * HD + HD])
        new_v.append(qkv[:, HEADS_TP * HD + HD :])
        for b in range(rolls):
            q = jnp.concatenate(
                [qkv[b : b + 1, h * HD : (h + 1) * HD] for h in range(HEADS_TP)], axis=0
            )
            scores = exact_dot(q, cache_ref[b, :, :HD], NT) * factor
            pos = lax.broadcasted_iota(jnp.int32, scores.shape, 1)
            scores = jnp.where(pos < lens_ref[b], scores, -1e30)
            extra = [
                jnp.sum(q * k[b : b + 1], axis=-1, keepdims=True) * factor for k in new_k
            ]
            top = jnp.max(scores, axis=-1, keepdims=True)
            for e in extra:
                top = jnp.maximum(top, e)
            expo = jnp.exp(scores - top)
            ee = [jnp.exp(e - top) for e in extra]
            den = jnp.sum(expo, axis=-1, keepdims=True)
            for e in ee:
                den = den + e
            att = jnp.dot(
                (expo / den).astype(BF16), cache_ref[b, :, HD:], preferred_element_type=F32
            )
            for e, v in zip(ee, new_v):
                att = att + (e / den).astype(BF16).astype(F32) * v[b : b + 1]
            att = att.astype(BF16).astype(F32)
            asend[step, b : b + 1, :] = jnp.concatenate(
                [att[h : h + 1] for h in range(HEADS_TP)], axis=1
            )
        dp_start(5 + 2 * step, lambda p: asend.at[step], arecv.at[step])
        bulk(1, 1)
        arecv[step, d] = asend[step]
        if step == 0:
            tp_start(2, lbsend, lbrecv)
            lbrecv[t] = lbsend[...]
        else:
            tp_wait(2, lbsend, lbrecv)
            lb = lbrecv[0]
            for i in range(1, ntp):
                lb = lb + lbrecv[i]
            lb = lb.astype(BF16)
            low_t, back_t = lb[0], lb[1]
            ga = adapter_scale * jnp.dot(back_t, x_ref[...], preferred_element_type=F32)
            gb = adapter_scale * jnp.dot(low_t, wt_ref[...], preferred_element_type=F32)
            for i in range(ndp):
                gsend[i, 0] = ga[:, i * piece : (i + 1) * piece]
                gsend[i, 1] = gb[:, i * piece : (i + 1) * piece]
        dp_wait(5 + 2 * step, lambda p: asend.at[step], arecv.at[step])
        attended = rows_of(arecv.at[step], ndp).astype(BF16)
        usend[step, :, :width] = jnp.dot(attended, wo_ref[...], preferred_element_type=F32)
        usend[step, :, width:] = jnp.concatenate(
            [
                lax.dot_general(attended, at, NT, preferred_element_type=F32),
                jnp.zeros((ndp * rolls, 128 - rank), F32),
            ],
            axis=1,
        )
        tp_start(step, usend.at[step], urecv.at[step])
        bulk(1, 1)
        urecv[step, t] = usend[step]
        if step == 0:
            src_t = d // half
            for j in range(per):
                frm = (d % half) * per + j
                same = jnp.logical_and(src_t == t, frm == d)

                @pl.when(jnp.logical_not(same))
                def _():
                    send(b_ref, bdbuf.at[j], bd_s.at[0], bd_r.at[j], (frm, src_t)).wait_recv()

            bd = lanes_of(bdbuf, per)
        tp_wait(step, usend.at[step], urecv.at[step])
        upd = urecv[step, 0]
        for i in range(1, ntp):
            upd = upd + urecv[step, i]
        state = state + (
            upd[:, :width] + adapter_scale * exact_dot(upd[:, width : width + rank], bd)
        )

    for i in range(ndp):
        fsend[i] = state[i * rolls : (i + 1) * rolls]
    dp_start(8, lambda p: fsend.at[p], frecv)
    frecv[d] = fsend[d]
    dp_start(9, lambda p: gsend.at[p], grecv)
    grecv[d] = gsend[d]
    bulk(len(pending), len(row_parts))
    rows_whole().wait_recv()
    relay(c).start()
    out_ref[...] = adapter_scale * lax.dot_general(low_t, bt, TN, preferred_element_type=F32)
    send(x_ref, xbuf.at[y, 1 - c], xs_s.at[0], xs_r.at[0], (d, mate)).wait_recv()
    dp_wait(8, lambda p: fsend.at[p], frecv)
    for i in range(ndp):
        dec_ref[:, i * width : (i + 1) * width] = frecv[i]
    relay(1 - c).wait_recv()

    def share(dx, dy, ch):
        zz = jnp.where(dx == 1, 1 - x, x)
        yy = jnp.where(dy == 1, 1 - y, y)
        return send(
            pbuf.at[dx, dy, ch],
            prcv.at[dx, dy, ch],
            ps_s.at[dx, dy, ch],
            ps_r.at[dx, dy, ch],
            (2 * z + yy, 2 * zz + c),
        )

    def stage(q, _):
        ch, r = q // 4, q % 4
        dx, dy = 1 - r // 2, 1 - r % 2
        zz = jnp.where(dx == 1, 1 - x, x)
        yy = jnp.where(dy == 1, 1 - y, y)

        @pl.when(dy == 1)
        def _():
            for cc in range(2):
                mine = jnp.logical_and(c + 2 * zz == z, c == cc)

                @pl.when(jnp.logical_not(mine))
                def _():
                    send(
                        wo_ref.at[:, pl.ds(0, CHUNK)],
                        wbuf.at[zz, cc, ch],
                        wl_s.at[0, 0],
                        wl_r.at[zz, cc, ch],
                        (d, mate),
                    ).wait_recv()

        p = jnp.dot(xbuf[yy, 0], wbuf[zz, 0, ch], preferred_element_type=F32)
        p = p + jnp.dot(xbuf[yy, 1], wbuf[zz, 1, ch], preferred_element_type=F32)
        last = r == 3

        @pl.when(jnp.logical_not(last))
        def _():
            pbuf[dx, dy, ch] = p
            share(dx, dy, ch).start()

        @pl.when(last)
        def _():
            cols = pl.ds(pl.multiple_of((y * chunks + ch) * CHUNK, CHUNK), CHUNK)
            out_ref[:, cols] += p

        return 0

    lax.fori_loop(0, 4 * chunks, stage, 0)

    dp_wait(9, lambda p: gsend.at[p], grecv)
    g = grecv[0]
    for i in range(1, ndp):
        g = g + grecv[i]
    ga_ref[...] = g[0]
    gb_ref[...] = g[1]
    for ch in range(chunks):
        for dx, dy in ((1, 0), (0, 1), (1, 1)):
            share(dx, dy, ch).wait_recv()
            yy = (y + dy) % 2
            cols = pl.ds(pl.multiple_of((yy * chunks + ch) * CHUNK, CHUNK), CHUNK)
            out_ref[:, cols] += prcv[dx, dy, ch]

    whole = pl.ds(0, wo_ref.shape[0])
    for ch in range(chunks):
        for off in range(1, nz):
            line(ch, off, whole).wait_send()

        @pl.when(z % 2 != c)
        def _():
            line(ch, 0, whole).wait_send()

        for dx, dy in ((1, 0), (0, 1), (1, 1)):
            share(dx, dy, ch).wait_send()
    rows_whole().wait_send()
    relay(c).wait_send()

    @pl.when(bdst != d)
    def _():
        send(b_ref, bdbuf.at[bslot], bd_s.at[0], bd_r.at[bslot], (bdst, t)).wait_send()

    for cp in sent:
        cp.wait_send()


def fused_shards(
    ndp,
    ntp,
    hidden,
    attention_norm_gain,
    query_key_value_weight,
    key_value_cache,
    cache_fill_lengths,
    output_weight_frozen,
    adapter_down_transposed,
    adapter_up_matrix,
    attention_rows,
    upstream,
    rewards,
    prompt_group_index,
    completion_live_lengths,
):
    rolls, model = hidden.shape
    width = model // ndp
    rank, _, piece = adapter_down_transposed.shape
    rows, shard = attention_rows.shape
    qkvw = query_key_value_weight.shape[2]
    feats = output_weight_frozen.shape[1]
    chunks = width // CHUNK
    vm = pl.BlockSpec(memory_space=pltpu.VMEM)
    sm = pl.BlockSpec(memory_space=pltpu.SMEM)
    dma = pltpu.SemaphoreType.DMA
    V = pltpu.VMEM
    dec, out, ga, gb = pl.pallas_call(
        lambda *refs: fused_kernel(ndp, ntp, *refs),
        out_shape=(
            jax.ShapeDtypeStruct((rolls, model), F32),
            jax.ShapeDtypeStruct((rows, shard), F32),
            jax.ShapeDtypeStruct((rank, piece), F32),
            jax.ShapeDtypeStruct((rank, piece), F32),
        ),
        in_specs=[vm, vm, vm, vm, sm, vm, vm, vm, vm, vm, sm, sm, sm],
        out_specs=(vm, vm, vm, vm),
        scratch_shapes=[
            V((ndp, rolls, width), F32),
            V((8, 128), F32),
            V((ndp, rolls, width), F32),
            V((ndp, rank, piece), BF16),
            V((ndp, rank, piece), BF16),
            V((width // piece, rank, piece), BF16),
            V((ndp, 8, 128), F32),
            V((2, ndp, rolls, qkvw + 128), F32),
            V((2, ndp, rolls, qkvw + 128), F32),
            V((2, rolls, feats), F32),
            V((2, ndp, rolls, feats), F32),
            V((2, ndp * rolls, width + 128), F32),
            V((2, ntp, ndp * rolls, width + 128), F32),
            V((ndp, rolls, width), F32),
            V((ndp, rolls, width), F32),
            V((2, rank, rows), F32),
            V((ntp, 2, rank, rows), F32),
            V((ndp, 2, rank, piece), F32),
            V((ndp, 2, rank, piece), F32),
            V((rows, shard), BF16),
            V((2, 2, rows, shard), BF16),
            V((2, 2, chunks, feats, CHUNK), BF16),
            V((2, 2, chunks, rows, CHUNK), F32),
            V((2, 2, chunks, rows, CHUNK), F32),
            dma((10, ndp)),
            dma((10, ndp)),
            dma((3, ntp)),
            dma((3, ntp)),
            dma((ntp,)),
            dma((width // piece,)),
            dma((3,)),
            dma((3,)),
            dma((chunks, ndp // 2)),
            dma((2, 2, chunks)),
            dma((2, 2, chunks)),
            dma((2, 2, chunks)),
        ],
        compiler_params=pltpu.CompilerParams(
            collective_id=0, has_side_effects=True, vmem_limit_bytes=60 * 2**20
        ),
    )(
        hidden,
        attention_norm_gain.reshape(1, model),
        query_key_value_weight[:, 0, :],
        key_value_cache[:, :, 0, :],
        cache_fill_lengths,
        output_weight_frozen[0],
        adapter_down_transposed[:, 0, :],
        adapter_up_matrix[:, 0, :],
        attention_rows,
        upstream,
        rewards,
        prompt_group_index,
        completion_live_lengths,
    )
    return dec, out, ga[:, None, :], gb[:, None, :]


def shards(
    hidden,
    attention_norm_gain,
    query_key_value_weight,
    key_value_cache,
    cache_fill_lengths,
    output_weight_frozen,
    adapter_down_transposed,
    adapter_up_matrix,
    attention_rows,
    upstream,
    rewards,
    prompt_group_index,
    completion_live_lengths,
):
    a_piece, b_piece = (
        lax.all_gather(adapter_down_transposed, "dp", axis=2, tiled=True),
        lax.all_gather(adapter_up_matrix, "dp", axis=2, tiled=True),
    )
    b_whole = lax.all_gather(b_piece, "tp", axis=1, tiled=True)
    up_matrix_flat = b_whole.reshape(b_whole.shape[0], -1).astype(jnp.float32)
    a_local = a_piece[:, 0, :]
    up_matrix_columns = b_piece[:, 0, :]
    w_rows = query_key_value_weight[:, 0, :].astype(jnp.float32)
    w_cols = output_weight_frozen[0]
    query_width = HEADS_TP * HD
    local_rolls = hidden.shape[0]
    decode_state = hidden.astype(jnp.float32)
    keys_new = []
    values_new = []
    for step in range(2):
        normed = rms_norm(decode_state, attention_norm_gain)
        spread = lax.all_to_all(normed, "dp", split_axis=1, concat_axis=0, tiled=True)
        partial_value = jnp.dot(spread, w_rows, precision=lax.Precision.HIGHEST)
        qkv = lax.psum_scatter(partial_value, "dp", scatter_dimension=0, tiled=True)
        query = qkv[:, :query_width].reshape(local_rolls, HEADS_TP, HD)
        keys_new.append(qkv[:, query_width : query_width + HD])
        values_new.append(qkv[:, query_width + HD :])
        attended = attend(
            query,
            key_value_cache[:, :, 0, :],
            cache_fill_lengths,
            jnp.stack(keys_new, axis=1),
            jnp.stack(values_new, axis=1),
        )
        columns = jnp.dot(
            lax.all_gather(attended, "dp", axis=0, tiled=True),
            w_cols,
            preferred_element_type=jnp.float32,
        )
        returned_values = lax.all_to_all(columns, "dp", split_axis=0, concat_axis=1, tiled=True)
        low_rank_decode = jnp.dot(attended, a_local.T, preferred_element_type=jnp.float32)
        state_update = returned_values + adapter_scale * jnp.dot(
            low_rank_decode, up_matrix_flat, precision=lax.Precision.HIGHEST
        )
        decode_state = decode_state + lax.psum(state_update, "tp")
    groups = local_rolls * lax.axis_size("dp") // GROUP
    onehot = (prompt_group_index[:, None] == jnp.arange(groups, dtype=jnp.int32)[None, :]).astype(
        jnp.float32
    )
    totals, squares = lax.psum(
        (
            jnp.sum(onehot * rewards[:, None], axis=0),
            jnp.sum(onehot * (rewards * rewards)[:, None], axis=0),
        ),
        "dp",
    )
    mean = totals / GROUP
    std = jnp.sqrt(jnp.maximum(squares / GROUP - mean * mean, 0.09))
    advantage = (rewards - jnp.sum(onehot * mean[None, :], axis=1)) / jnp.sum(
        onehot * std[None, :], axis=1
    )
    per_roll = advantage / completion_live_lengths.astype(jnp.float32)
    rows = attention_rows.shape[0]
    slot = jnp.arange(rows, dtype=jnp.int32) % COMP
    limit = jnp.repeat(completion_live_lengths, COMP)
    row_w = jnp.where(slot < limit, jnp.repeat(per_roll, COMP), 0.0)
    whole_rows = jnp.dot(
        attention_rows,
        lax.all_gather(output_weight_frozen, "dp", axis=2, tiled=True)[0],
        preferred_element_type=jnp.float32,
    )
    frozen_output_rows = lax.psum_scatter(whole_rows, "tp", scatter_dimension=1, tiled=True)
    low_sum = lax.psum(jnp.dot(attention_rows, a_local.T, preferred_element_type=jnp.float32), "tp")
    low_rank_rows = low_sum.astype(jnp.bfloat16)
    adapted_output_rows = frozen_output_rows + adapter_scale * jnp.dot(
        low_rank_rows, up_matrix_columns, preferred_element_type=jnp.float32
    )
    advantage_weighted = (row_w[:, None] * upstream.astype(jnp.float32)).astype(jnp.bfloat16)
    backward_result = lax.psum(
        jnp.dot(advantage_weighted, up_matrix_columns.T, preferred_element_type=jnp.float32), "tp"
    ).astype(jnp.bfloat16)
    down_gradient = adapter_scale * lax.dot_general(
        backward_result,
        attention_rows,
        (((0,), (0,)), ((), ())),
        preferred_element_type=jnp.float32,
    )
    up_gradient = adapter_scale * lax.dot_general(
        low_rank_rows,
        advantage_weighted,
        (((0,), (0,)), ((), ())),
        preferred_element_type=jnp.float32,
    )
    grad_a_part, grad_b_part = (
        lax.psum_scatter(down_gradient[:, None, :], "dp", scatter_dimension=2, tiled=True),
        lax.psum_scatter(up_gradient[:, None, :], "dp", scatter_dimension=2, tiled=True),
    )
    return (decode_state, adapted_output_rows, grad_a_part, grad_b_part)


def solution(mesh):
    placed = (
        P("dp", None),
        P(),
        P("dp", "tp", None),
        P("dp", None, "tp", None),
        P("dp"),
        P("tp", None, "dp"),
        P(None, "tp", "dp"),
        P(None, "tp", "dp"),
        P("dp", "tp"),
        P("dp", "tp"),
        P("dp"),
        P("dp"),
        P("dp"),
    )
    ndp, ntp = mesh.shape["dp"], mesh.shape["tp"]

    def body(*args):
        width = args[5].shape[2]
        piece = args[6].shape[2]
        if ntp == 4 and ndp == 8 and piece % 128 == 0 and width % CHUNK == 0:
            return fused_shards(ndp, ntp, *args)
        return shards(*args)

    return jax.shard_map(
        body,
        mesh=mesh,
        in_specs=placed,
        out_specs=(P("dp", None), P("dp", "tp"), P(None, "tp", "dp"), P(None, "tp", "dp")),
        check_vma=False,
    )
```
